256 devices in a mesh: slab: 8 (over z), front: 32 (over y, x, core).
Axes of the slice: x: 4, y: 4, z: 8, core: 2. Of those that a mesh axis runs over, the one named last changes fastest.
Arguments:
- leaf_rhs: bfloat16 [8, 2, 512, 128, 512], P('slab', None, 'front'), may hold values from -6 to 6
- leaf_inv: bfloat16 [8, 512, 2, 128, 128], P('slab', 'front'), may hold values from -0.375 to 0.375
- leaf_off: bfloat16 [8, 512, 2, 128, 128], P('slab', 'front'), may hold values from -0.125 to 0.125
- parent: int32 [8, 512, 1], P('slab', 'front'), may hold values from 0 to 31; in each aligned block of 16 rows (0 to 15, 16 to 31, ..., all dimensions but the last counted through in order) no two rows name the same one
- ancestors: int32 [8, 512, 128], P('slab', 'front'), may hold values from 0 to 255
- root_rhs: bfloat16 [8, 2, 8192, 512], P('slab', None, 'front'), may hold values from -6 to 6
- root_inv: float32 [8, 64, 2, 128, 128], P('slab', 'front'), may hold values from -2 to 2.5
- coupling: float32 [8, 8192], P('slab', 'front'), may hold values from 0.6 to 1.3
Outputs:
- leaf_sol: bfloat16 [8, 2, 512, 128, 512], P('slab', None, 'front')
- root_sol: float32 [8, 2, 8192, 512], P('slab', None, 'front')
The draws below stay inside these ranges and needn't reach their ends.
Inputs may be any that keep to these rules, and one draw needn't show every extreme that they name: Each front index's 16 leaf blocks of a slab name any one parent at most 1 times. `ancestors`: rows may repeat within a block.
All inputs are finite; a program needn't handle non-finite values.
Results may differ from the reference program's by a relative error of at most 0.0057.
Values may be sent and summed in bfloat16 or wider, within the bound.
A program may use at most 128 MiB of HBM per device.

```python
import math
import jax
import jax.numpy as jnp
import numpy as np
from jax import lax

BLK = 128
ROOT_DEV = 256
LEAF_DEV = 16
SLABS = 8
LEAVES = 512
TRACE = 8192
PCOLS = 512
CAP = 1
N_FRONT = 32


def draw_root_inv(key, part):
    shape = (SLABS, TRACE // BLK, 2, BLK, BLK)
    noise = jax.random.truncated_normal(key, -4.0, 4.0, shape, jnp.float32)
    eye = jnp.eye(BLK, dtype=jnp.float32)
    diagonal = jnp.stack([0.8 * eye, 0.0 * eye])
    return diagonal + noise * (0.35 / BLK ** 0.5)


def plant(values, own_key, low, top_value):
    index_at = [jax.random.randint(jax.random.fold_in(own_key, axis), (), 0, length) for axis, length in enumerate(values.shape)]
    widest = values.shape.index(max(values.shape))
    neighbour = index_at[:widest] + [(index_at[widest] + 1) % values.shape[widest]] + index_at[widest + 1:]
    return values.at[tuple(index_at)].set(low).at[tuple(neighbour)].set(top_value)


def steps_of(rng, dims, cuts, low, top_value):
    gain = 1.0
    for position, parts in cuts:
        heights = jax.random.uniform(jax.random.fold_in(jax.random.fold_in(rng, 6), position), (parts,), jnp.float32, low / len(cuts), top_value / len(cuts))
        gain = gain * jnp.repeat(jnp.exp(heights), dims[position] // parts).reshape((-1,) + (1,) * (len(dims) - 1 - position))
    return gain


def rank_table(amount, slope):
    loads = [(1 << 20) // math.isqrt(rank ** slope) + 1 for rank in range(1, amount + 1)]
    spread = 1 + sum(loads) // (1 << 30)
    return np.cumsum(np.array([max(1, weight // spread) for weight in loads]))


def ranked(own_key, dims, amount, lean):
    listing = rank_table(amount, lean)
    lot = jax.random.randint(jax.random.fold_in(own_key, 1), dims, 0, int(listing[amount - 1]))
    grade = jnp.searchsorted(jnp.asarray(listing, jnp.int32), lot, side="right")
    return jax.random.permutation(jax.random.fold_in(own_key, 2), amount)[grade].astype(jnp.int32)


def routed_block(rng, own, number, rows, count, top, most, lean):
    sequence = jax.random.permutation(rng, count)
    packed, ordinary = load_shares(count, rows * top, most, lean, True), load_shares(count, rows * top, most, lean, False)
    places = jnp.arange(count)

    def named(sizes, turn):
        used = int((sizes > 0).sum())
        fixed = max(1, used // 4)
        passed = fixed + (places - fixed + turn * (used - fixed)) % max(1, count - fixed)
        return jnp.zeros((count,), jnp.int32).at[sequence[jnp.where(places < fixed, places, passed)]].set(jnp.asarray(sizes, jnp.int32))

    sizes = jnp.where(number % 4 == 0, named(packed, number // 4), named(ordinary, number - number // 4 - 1))
    mixed = jax.random.permutation(jax.random.fold_in(own, 3), count)
    giver, taker = mixed[0:count // 2 * 2:2], mixed[1:count // 2 * 2:2]
    slack = jnp.minimum(sizes[giver] - 1, most - sizes[taker]) // 2
    slack = jnp.where((giver == sequence[0]) | (taker == sequence[0]) | (sizes[taker] == 0), 0, jnp.maximum(slack, 0))
    passed = jax.random.randint(jax.random.fold_in(own, 4), (count // 2,), 0, 1 << 20) % (slack + 1)
    sizes = sizes.at[giver].add(-passed).at[taker].add(passed)
    items = jnp.searchsorted(jnp.cumsum(sizes), jnp.arange(rows * top), side="right").astype(jnp.int32)
    table = items.reshape(top, rows).T
    table = table[jax.random.permutation(jax.random.fold_in(own, 1), rows)]
    turn = jax.random.randint(jax.random.fold_in(own, 2), (rows, 1), 0, top)
    return jnp.take_along_axis(table, (jnp.arange(top)[None, :] + turn) % top, axis=1)


def load_shares(count, total, most, skew, full):
    portions = [(1 << 20) // math.isqrt(standing ** skew) + 1 for standing in range(1, count + 1)]
    largest = most if full else min(most, max(-(-total // count), total * portions[0] // sum(portions)))
    least = 1 if total - largest >= count - 1 else 0
    given, surplus = [largest] + [least] * (count - 1), total - largest - least * (count - 1)
    while surplus > 0:
        candidates = [i for i in range(1, count) if given[i] < largest] or [i for i in range(1, count) if given[i] < most]
        pool, budget = sum([portions[i] for i in candidates]), surplus
        for i in candidates:
            extra = min(most - given[i], max(1, budget * portions[i] // pool), surplus)
            given[i] = given[i] + extra
            surplus = surplus - extra
    return np.array(given)


def centred(rng, shape, deviation, reach, pieces=(), held_as=jnp.bfloat16):
    factor_of = steps_of(rng, shape, pieces, -0.22, 0.18) if pieces else 1.0
    drawn = jax.random.normal(rng, shape, jnp.float32) * deviation * factor_of
    return jnp.minimum(jnp.maximum(drawn, -reach), reach).astype(held_as)


def setup_inputs(seed: int = 0) -> dict:
    key_of = jax.random.split(jax.random.key(seed), 9)
    leaf_rhs = centred(key_of[0], (SLABS, 2, LEAVES, BLK, PCOLS), 1.0, 6.0, ((0, 8), (2, 32)))
    leaf_inv = centred(key_of[1], (SLABS, LEAVES, 2, BLK, BLK), (2 * BLK) ** -0.5, 0.375, ((0, 8), (1, 32)))
    leaf_off = centred(key_of[2], (SLABS, LEAVES, 2, BLK, BLK), (16 * BLK) ** -0.5, 0.125, ((0, 8), (1, 32)))
    parent_keys = jax.random.split(jax.random.fold_in(key_of[3], 1), SLABS * LEAVES // LEAF_DEV)
    parent_turns = jax.random.permutation(jax.random.fold_in(key_of[3], 3), SLABS * LEAVES // LEAF_DEV)
    parent = jax.vmap(lambda own, number: routed_block(jax.random.fold_in(key_of[3], 2), own, number, LEAF_DEV, N_FRONT, 1, CAP, 2))(parent_keys, parent_turns).reshape((SLABS, LEAVES, 1))
    ancestors = plant(ranked(key_of[4], (SLABS, LEAVES, BLK), ROOT_DEV, 1), jax.random.fold_in(key_of[4], 3), 0, ROOT_DEV - 1).astype(jnp.int32)
    root_rhs = centred(key_of[5], (SLABS, 2, TRACE, PCOLS), 1.0, 6.0, ((0, 8), (2, 32)))
    root_inv = draw_root_inv(jax.random.fold_in(key_of[8], 71), 0)
    coupling = jnp.clip(jnp.exp(math.log(1.3) - 0.7731898 * jax.random.uniform(key_of[7], (SLABS, TRACE), jnp.float32) ** steps_of(key_of[7], (SLABS, TRACE), ((0, 8), (1, 32)), -0.2, 0.2)), 0.6, 1.3)
    return {"leaf_rhs": leaf_rhs, "leaf_inv": leaf_inv, "leaf_off": leaf_off, "parent": parent, "ancestors": ancestors, "root_rhs": root_rhs, "root_inv": root_inv, "coupling": coupling}


def cplx(mat, vec, form):
    real = jnp.einsum(form, mat[:, 0], vec[0]) - jnp.einsum(form, mat[:, 1], vec[1])
    imag = jnp.einsum(form, mat[:, 0], vec[1]) + jnp.einsum(form, mat[:, 1], vec[0])
    return jnp.stack([real, imag])


def block_solve(blocks, field):
    highest = lax.Precision.HIGHEST
    shaped = field.reshape(2, blocks.shape[0], blocks.shape[2], field.shape[-1])
    real = jnp.einsum("kij,kjc->kic", blocks[:, 0], shaped[0], precision=highest) - jnp.einsum("kij,kjc->kic", blocks[:, 1], shaped[1], precision=highest)
    imag = jnp.einsum("kij,kjc->kic", blocks[:, 0], shaped[1], precision=highest) + jnp.einsum("kij,kjc->kic", blocks[:, 1], shaped[0], precision=highest)
    return jnp.stack([real, imag]).reshape(field.shape)


def reference(leaf_rhs, leaf_inv, leaf_off, parent, ancestors, root_rhs, root_inv, coupling):
    forward_form = "lij,ljc->lic"
    back_form = "lji,ljc->lic"

    def leaf_forward(item):
        rhs, inv, off, par, anc, right = item
        fwd = lax.optimization_barrier(cplx(inv.astype(jnp.float32), rhs.astype(jnp.float32), forward_form).astype(jnp.bfloat16))
        part = lax.optimization_barrier(cplx(off.astype(jnp.float32), fwd.astype(jnp.float32), forward_form).astype(jnp.bfloat16))
        rows = (par[:, 0:1] * ROOT_DEV + anc).astype(jnp.int32).reshape(-1)
        flat = part.astype(jnp.float32).reshape(2, -1, PCOLS)
        summed = jnp.zeros((2, TRACE, PCOLS), jnp.float32).at[:, rows].add(flat)
        return fwd, right.astype(jnp.float32) - summed

    fwd_all, reduced = lax.map(leaf_forward, (leaf_rhs, leaf_inv, leaf_off, parent, ancestors, root_rhs))

    def link(previous, item):
        right, blocks, cpl = item
        state = block_solve(blocks, right - cpl[None, :, None] * previous)
        return state, state

    start = jnp.zeros((2, TRACE, PCOLS), jnp.float32)
    _, roots = lax.scan(link, start, (reduced, root_inv, coupling))

    def leaf_back(item):
        fwd, inv, off, par, anc, root = item
        half = lax.optimization_barrier(root.astype(jnp.bfloat16))
        rows = (par[:, 0:1] * ROOT_DEV + anc).astype(jnp.int32).reshape(-1)
        picked = half.astype(jnp.float32)[:, rows].reshape(2, LEAVES, BLK, PCOLS)
        back = lax.optimization_barrier(cplx(off.astype(jnp.float32), picked, back_form).astype(jnp.bfloat16))
        return (fwd.astype(jnp.float32) - cplx(inv.astype(jnp.float32), back.astype(jnp.float32), forward_form)).astype(jnp.bfloat16)

    leaves = lax.map(leaf_back, (fwd_all, leaf_inv, leaf_off, parent, ancestors, roots))
    return leaves, roots
```

```python
import jax
import jax.numpy as jnp
from jax import lax
from jax.experimental import pallas as pl
from jax.experimental.pallas import tpu as pltpu
from jax.sharding import PartitionSpec as P

BF = jnp.bfloat16
F32 = jnp.float32
B = 128
C = 128
LEAF = 16
RING = 4
SLOTS = RING * RING
MESSAGES = 52
LAG_NUM, LAG_DEN = 3, 8
STEPS_AFTER = 10


def dot(a, b):
    return jnp.dot(a, b, preferred_element_type=F32)


def widened(real, imag):
    top = jnp.concatenate([real, -imag], axis=1)
    low = jnp.concatenate([imag, real], axis=1)
    return jnp.concatenate([top, low], axis=0)


def kernel(
    slot_leaf, leaf_slot, rhs, inv, off, ids, root_rhs, root_inv, cpl,
    sol_out, root_out,
    X, PART, SND, RCV, IDR, T, TT, OFFT, E, A1, F1, R1, A2, F2, RR, AH, AL, Z, Y, G, RCB, STAGE,
    ssem, rsem, idsem, insem, rrsem, outsem, rootsem,
):
    slabs = lax.axis_size("slab")
    chunks = X.shape[0]
    slab = lax.axis_index("slab")
    front = lax.axis_index("front")
    core = front % 2
    chip = front // 2
    cx = chip % RING
    cy = chip // RING

    def at(x, y, c):
        return (slab, (y * RING + x) * 2 + c)

    partner = at(cx, cy, 1 - core)
    x_next = at((cx + 1) % RING, cy, core)
    x_prev = at((cx + RING - 1) % RING, cy, core)
    y_next = at(cx, (cy + 1) % RING, core)
    y_prev = at(cx, (cy + RING - 1) % RING, core)
    z_next = ((slab + 1) % slabs, front)
    z_prev = ((slab + slabs - 1) % slabs, front)
    ways = ((x_next, x_prev), (y_next, y_prev))

    barrier = pltpu.get_barrier_semaphore()
    for device in (partner, x_next, x_prev, y_next, y_prev, z_next, z_prev):
        pl.semaphore_signal(barrier, inc=1, device_id=device, device_id_type=pl.DeviceIdType.MESH)

    def cols(k):
        return pl.ds(pl.multiple_of(k * C, C), C)

    def rhs_in(k):
        return pltpu.make_async_copy(rhs.at[0, :, :, :, cols(k)], X.at[k], insem.at[k])

    def root_rhs_in(k):
        return pltpu.make_async_copy(root_rhs.at[0, :, :, cols(k)], RR.at[k], rrsem.at[k])

    def sol_back(k):
        return pltpu.make_async_copy(X.at[k], sol_out.at[0, :, :, :, cols(k)], outsem.at[k])

    def root_back(k):
        return pltpu.make_async_copy(Y.at[k], root_out.at[0, :, :, cols(k)], rootsem.at[k])

    for k in range(chunks):
        rhs_in(k).start()
        root_rhs_in(k).start()

    def send(src, dst, k, m, device):
        return pltpu.make_async_remote_copy(
            src_ref=src, dst_ref=dst, send_sem=ssem.at[k, m], recv_sem=rsem.at[k, m],
            device_id=device, device_id_type=pl.DeviceIdType.MESH,
        )

    def ids_copy():
        return pltpu.make_async_remote_copy(
            src_ref=ids.at[1], dst_ref=IDR, send_sem=idsem.at[0], recv_sem=idsem.at[1],
            device_id=partner, device_id_type=pl.DeviceIdType.MESH,
        )

    def part_copy(k):
        return send(SND.at[k], RCV.at[k], k, 0, partner)

    def rs_copy(k, p, phase, m):
        nxt, prv = ways[p if phase == 0 else 1 - p]
        if phase == 0:
            src, mid, fin = E, A1, F1
        else:
            src, mid, fin = R1, A2, F2
        s, d, device = (
            (src.at[k, p, 2, 0], mid.at[k, p, 0], nxt),
            (src.at[k, p, 1, 1], fin.at[k, p, 0, 1], nxt),
            (src.at[k, p, 1, 0], fin.at[k, p, 0, 0], nxt),
            (src.at[k, p, 2, 1], mid.at[k, p, 1], prv),
            (src.at[k, p, 3, 0], fin.at[k, p, 1, 0], prv),
            (src.at[k, p, 3, 1], fin.at[k, p, 1, 1], prv),
        )[m]
        return send(s, d, k, 1 + phase * 12 + p * 6 + m, device)

    def sweep_copy(k, b):
        return send(G.at[k, :, 0, b, 0], Z.at[k, b], k, 25 + b, z_next)

    def ag_copy(k, p, phase, m):
        nxt, prv = ways[1 - p if phase == 0 else p]
        if phase == 0:
            def g(r, h):
                return G.at[k, p, 0, h, r]
        else:
            def g(r, h):
                return G.at[k, p, r, h]
        s, d, device = (
            (g(0, 0), g(3, 0), nxt),
            (g(0, 1), g(3, 1), nxt),
            (g(3, 0), g(2, 0), nxt),
            (g(0, 1), g(1, 1), prv),
            (g(0, 0), g(1, 0), prv),
            (g(1, 1), g(2, 1), prv),
        )[m]
        return send(s, d, k, 27 + phase * 12 + p * 6 + m, device)

    def pick_copy(k):
        return send(SND.at[k], RCB.at[k], k, 51, partner)

    @pl.when(slab == 0)
    def _():
        Z[...] = jnp.zeros_like(Z)

    pl.semaphore_wait(barrier, 7)
    ids_copy().start()

    for b in range(2):
        full = widened(root_inv[0, b, 0], root_inv[0, b, 1])
        high = full.astype(BF)
        AH[b] = high
        AL[b] = (full - high.astype(F32)).astype(BF)

    def fwd(k):
        rhs_in(k).wait()
        par = k % 2

        def leaf(l, carry):
            v = jnp.concatenate([X[k, 0, l], X[k, 1, l]], axis=0)
            f = dot(widened(inv[0, l, 0], inv[0, l, 1]), v).astype(BF)
            X[k, 0, l] = f[:B]
            X[k, 1, l] = f[B:]
            w = dot(widened(off[0, l, 0], off[0, l, 1]), f).astype(BF)
            PART[par, l, 0] = w[:B]
            PART[par, l, 1] = w[B:]
            return carry

        lax.fori_loop(0, LEAF, leaf, 0, unroll=2)

        def put(q, carry):
            SND[k, q] = PART[par, slot_leaf[SLOTS + q]]
            return carry

        lax.fori_loop(0, SLOTS, put, 0, unroll=2)
        part_copy(k).start()

    def setup_tables():
        ids_copy().wait_recv()

        def table(q, carry):
            both = jnp.concatenate([ids[0, pl.ds(q, 1), :], IDR[pl.ds(q, 1), :]], axis=1)
            rows = lax.broadcasted_iota(jnp.int32, (2 * B, 2 * B), 0)
            T[q] = jnp.where(rows == jnp.broadcast_to(both, (2 * B, 2 * B)), 1.0, 0.0).astype(BF)
            return carry

        lax.fori_loop(0, SLOTS, table, 0)

    def setup_transposed():
        def table(q, carry):
            TT[q] = T[q].astype(F32).T.astype(BF)
            OFFT[q] = widened(off[0, q, 0].astype(F32).T, off[0, q, 1].astype(F32).T).astype(BF)
            return carry

        lax.fori_loop(0, SLOTS, table, 0)

    def expand(k):
        part_copy(k).wait_recv()
        par = k % 2

        def slot(q, carry):
            rx, ry = q // RING, q % RING
            leaf = slot_leaf[q]
            v = jnp.concatenate(
                [
                    jnp.concatenate([PART[par, leaf, 0], PART[par, leaf, 1]], axis=1),
                    jnp.concatenate([RCV[k, q, 0], RCV[k, q, 1]], axis=1),
                ],
                axis=0,
            )
            e = dot(T[q], v).astype(BF)
            E[k, 0, rx, 0, ry] = e[:B, :C]
            E[k, 0, rx, 1, ry] = e[B:, :C]
            E[k, 1, ry, 0, rx] = e[:B, C:]
            E[k, 1, ry, 1, rx] = e[B:, C:]
            return carry

        lax.fori_loop(0, SLOTS, slot, 0, unroll=2)
        for m in (0, 3, 1, 4):
            for p in range(2):
                rs_copy(k, p, 0, m).start()

    def rs_relay_first(k):
        for m, r, h, d in ((0, 1, 0, 0), (3, 3, 1, 1)):
            for p in range(2):
                rs_copy(k, p, 0, m).wait_recv()
                for i in range(RING):
                    E[k, p, r, h, i] = (
                        E[k, p, r, h, i].astype(F32) + A1[k, p, d, i].astype(F32)
                    ).astype(BF)
                rs_copy(k, p, 0, 2 if d == 0 else 5).start()

    def rs_turn(k):
        for p in range(2):
            for m in (1, 4, 2, 5):
                rs_copy(k, p, 0, m).wait_recv()
            for r in (2, 1, 3, 0):
                for h in range(2):
                    R1[k, p, r, h] = (
                        E[k, p, 0, h, r].astype(F32)
                        + F1[k, p, 0, h, r].astype(F32)
                        + F1[k, p, 1, h, r].astype(F32)
                    ).astype(BF)
            for m in (0, 3, 1, 4):
                rs_copy(k, p, 1, m).start()

    def rs_relay_second(k):
        for m, r, h, d in ((0, 1, 0, 0), (3, 3, 1, 1)):
            for p in range(2):
                rs_copy(k, p, 1, m).wait_recv()
                R1[k, p, r, h] = (
                    R1[k, p, r, h].astype(F32) + A2[k, p, d].astype(F32)
                ).astype(BF)
                rs_copy(k, p, 1, 2 if d == 0 else 5).start()

    def sweep(k):
        root_rhs_in(k).wait()
        for p in range(2):
            for m in (1, 4, 2, 5):
                rs_copy(k, p, 1, m).wait_recv()
        for b in range(2):
            right = []
            for p in range(2):
                total = (
                    R1[k, p, 0, b].astype(F32)
                    + F2[k, p, 0, b].astype(F32)
                    + F2[k, p, 1, b].astype(F32)
                )
                right.append(RR[k, p, pl.ds(b * B, B), :].astype(F32) - total)

            @pl.when(slab > 0)
            def _():
                sweep_copy(k, b).wait_recv()

            scale = cpl[pl.ds(b * B, B), :]
            field = jnp.concatenate(
                [right[p] - scale * Z[k, b, p].astype(F32) for p in range(2)], axis=0
            )
            high = field.astype(BF)
            low = (field - high.astype(F32)).astype(BF)
            state = dot(AH[b], low) + dot(AL[b], high) + dot(AH[b], high)
            for p in range(2):
                piece = state[p * B:(p + 1) * B]
                G[k, p, 0, b, 0] = piece.astype(BF)
                Y[k, p, pl.ds(b * B, B), :] = piece

            @pl.when(slab < slabs - 1)
            def _():
                sweep_copy(k, b).start()

            for p in range(2):
                for m in ((0, 4), (3, 1))[b]:
                    ag_copy(k, p, 0, m).start()
        root_back(k).start()

    def ag_forward(k, phase):
        for m in (0, 3):
            for p in range(2):
                ag_copy(k, p, phase, m).wait_recv()
                ag_copy(k, p, phase, m + 2).start()

    def ag_turn(k):
        for p in range(2):
            for m in (1, 4, 2, 5):
                ag_copy(k, p, 0, m).wait_recv()
        for m in (0, 3, 1, 4):
            for p in range(2):
                ag_copy(k, p, 1, m).start()

    def pick(k):
        for p in range(2):
            for m in (1, 4, 2, 5):
                ag_copy(k, p, 1, m).wait_recv()
        part_copy(k).wait_send()

        def slot(q, carry):
            rx, ry = q // RING, q % RING
            v = jnp.concatenate(
                [
                    jnp.concatenate([G[k, 0, rx, 0, ry], G[k, 1, ry, 0, rx]], axis=1),
                    jnp.concatenate([G[k, 0, rx, 1, ry], G[k, 1, ry, 1, rx]], axis=1),
                ],
                axis=0,
            )
            e = dot(TT[q], v).astype(BF)
            STAGE[q, 0] = e[:B, :C]
            STAGE[q, 1] = e[:B, C:]
            SND[k, q, 0] = e[B:, :C]
            SND[k, q, 1] = e[B:, C:]
            return carry

        lax.fori_loop(0, SLOTS, slot, 0, unroll=2)
        pick_copy(k).start()

    def back(k):
        pick_copy(k).wait_recv()

        def put(q, carry):
            STAGE[SLOTS + q] = RCB[k, q]
            return carry

        lax.fori_loop(0, SLOTS, put, 0, unroll=2)

        def leaf(l, carry):
            s = leaf_slot[l]
            v = jnp.concatenate([STAGE[s, 0], STAGE[s, 1]], axis=0)
            w = dot(OFFT[l], v).astype(BF)
            u = dot(widened(inv[0, l, 0], inv[0, l, 1]), w)
            X[k, 0, l] = (X[k, 0, l].astype(F32) - u[:B]).astype(BF)
            X[k, 1, l] = (X[k, 1, l].astype(F32) - u[B:]).astype(BF)
            return carry

        lax.fori_loop(0, LEAF, leaf, 0, unroll=2)
        sol_back(k).start()

    lag = slab * LAG_NUM // LAG_DEN

    def step(j, carry):
        def run(op, shift, *rest):
            k = j - shift

            @pl.when((k >= 0) & (k < chunks))
            def _():
                op(k, *rest)

        run(fwd, 0)

        @pl.when(j == 1)
        def _():
            setup_tables()

        run(expand, 1)
        run(rs_relay_first, 2)

        @pl.when(j == 4)
        def _():
            setup_transposed()

        run(rs_turn, 3)
        run(rs_relay_second, 4)
        run(sweep, 5 + lag)
        run(ag_forward, 6 + lag, 0)
        run(ag_turn, 7 + lag)
        run(ag_forward, 8 + lag, 1)
        run(back, 10 + lag)
        run(pick, 9 + lag)
        return carry

    lax.fori_loop(0, chunks + STEPS_AFTER + (slabs - 1) * LAG_NUM // LAG_DEN, step, 0)

    ids_copy().wait_send()

    def drain(k, carry):
        sol_back(k).wait()
        root_back(k).wait()
        for phase in range(2):
            for p in range(2):
                for m in range(6):
                    rs_copy(k, p, phase, m).wait_send()
                    ag_copy(k, p, phase, m).wait_send()
        for b in range(2):
            @pl.when(slab < slabs - 1)
            def _():
                sweep_copy(k, b).wait_send()
        pick_copy(k).wait_send()
        return carry

    lax.fori_loop(0, chunks, drain, 0)


def body(leaf_rhs, leaf_inv, leaf_off, parent, ancestors, root_rhs, root_inv, coupling):
    owners = parent[0, :, 0]
    anc = ancestors[0]
    width = leaf_rhs.shape[-1]
    chunks = width // C
    front = lax.axis_index("front")
    core, chip = front % 2, front // 2
    cx, cy = chip % RING, chip // RING
    n = jnp.arange(2 * SLOTS, dtype=jnp.int32)
    cls, q = n // SLOTS, n % SLOTS
    dest_x = (cx + q // RING) % RING
    dest_y = (cy + q % RING) % RING
    dest = (dest_y * RING + dest_x) * 2 + (core + cls) % 2
    match = (owners[None, :] == dest[:, None]).astype(jnp.int32)
    slot_leaf = jnp.sum(match * jnp.arange(LEAF, dtype=jnp.int32)[None, :], axis=1)
    leaf_slot = jnp.sum(match * n[:, None], axis=0)
    ids = jnp.sum(match[:, :, None] * (anc[None] + 1), axis=1) - 1
    ids = ids.reshape(2, SLOTS, B)
    cpl = jnp.broadcast_to(coupling[0][:, None], (2 * B, C))
    vmem = pl.BlockSpec(memory_space=pltpu.VMEM)
    smem = pl.BlockSpec(memory_space=pltpu.SMEM)
    hbm = pl.BlockSpec(memory_space=pl.ANY)
    scratch = [
        pltpu.VMEM((chunks, 2, LEAF, B, C), BF),
        pltpu.VMEM((2, LEAF, 2, B, C), BF),
        pltpu.VMEM((chunks, SLOTS, 2, B, C), BF),
        pltpu.VMEM((chunks, SLOTS, 2, B, C), BF),
        pltpu.VMEM((SLOTS, B), jnp.int32),
        pltpu.VMEM((SLOTS, 2 * B, 2 * B), BF),
        pltpu.VMEM((SLOTS, 2 * B, 2 * B), BF),
        pltpu.VMEM((LEAF, 2 * B, 2 * B), BF),
        pltpu.VMEM((chunks, 2, RING, 2, RING, B, C), BF),
        pltpu.VMEM((chunks, 2, 2, RING, B, C), BF),
        pltpu.VMEM((chunks, 2, 2, 2, RING, B, C), BF),
        pltpu.VMEM((chunks, 2, RING, 2, B, C), BF),
        pltpu.VMEM((chunks, 2, 2, B, C), BF),
        pltpu.VMEM((chunks, 2, 2, 2, B, C), BF),
        pltpu.VMEM((chunks, 2, 2 * B, C), BF),
        pltpu.VMEM((2, 2 * B, 2 * B), BF),
        pltpu.VMEM((2, 2 * B, 2 * B), BF),
        pltpu.VMEM((chunks, 2, 2, B, C), BF),
        pltpu.VMEM((chunks, 2, 2 * B, C), F32),
        pltpu.VMEM((chunks, 2, RING, 2, RING, B, C), BF),
        pltpu.VMEM((chunks, SLOTS, 2, B, C), BF),
        pltpu.VMEM((2 * SLOTS, 2, B, C), BF),
        pltpu.SemaphoreType.DMA((chunks, MESSAGES)),
        pltpu.SemaphoreType.DMA((chunks, MESSAGES)),
        pltpu.SemaphoreType.DMA((2,)),
        pltpu.SemaphoreType.DMA((chunks,)),
        pltpu.SemaphoreType.DMA((chunks,)),
        pltpu.SemaphoreType.DMA((chunks,)),
        pltpu.SemaphoreType.DMA((chunks,)),
    ]
    return pl.pallas_call(
        kernel,
        out_shape=(
            jax.ShapeDtypeStruct(leaf_rhs.shape, BF),
            jax.ShapeDtypeStruct(root_rhs.shape, F32),
        ),
        in_specs=[smem, smem, hbm, vmem, vmem, vmem, hbm, vmem, vmem],
        out_specs=(hbm, hbm),
        scratch_shapes=scratch,
        compiler_params=pltpu.CompilerParams(
            collective_id=0, has_side_effects=True, vmem_limit_bytes=67043328
        ),
        name="sweep_all",
    )(slot_leaf, leaf_slot, leaf_rhs, leaf_inv, leaf_off, ids, root_rhs, root_inv, cpl)


def solution(mesh):
    in_specs = (
        P("slab", None, "front", None, None),
        P("slab", "front", None, None, None),
        P("slab", "front", None, None, None),
        P("slab", "front", None),
        P("slab", "front", None),
        P("slab", None, "front", None),
        P("slab", "front", None, None, None),
        P("slab", "front"),
    )
    out_specs = (P("slab", None, "front", None, None), P("slab", None, "front", None))
    return jax.shard_map(body, mesh=mesh, in_specs=in_specs, out_specs=out_specs, check_vma=False)
```

```python
import jax
import jax.numpy as jnp
from jax import lax
from jax.experimental import pallas as pl
from jax.experimental.pallas import tpu as pltpu
from jax.sharding import PartitionSpec as P

BF = jnp.bfloat16
F32 = jnp.float32
B = 128
C = 128
LEAF = 16
RING = 4
SLOTS = RING * RING
MESSAGES = 52
LAG_NUM, LAG_ADD, LAG_DEN = 2, 5, 7
GATHER = (6, 7, 8)
WIDE = 8


def dot(a, b):
    return jnp.dot(a, b, preferred_element_type=F32)


def widened(real, imag):
    top = jnp.concatenate([real, -imag], axis=1)
    low = jnp.concatenate([imag, real], axis=1)
    return jnp.concatenate([top, low], axis=0)


def kernel(
    owners, rhs, inv_in, off_in, anc, root_rhs, root_inv, coupling,
    sol_out, root_out,
    slot_leaf, leaf_slot, ids, inv, off, cpl,
    X, PART, SND, RCV, IDR, T, TT, OFFT, E, A1, F1, R1, A2, F2, RR, AH, AL, Z, Y, G, RCB, STAGE,
    ssem, rsem, idsem, insem, rrsem, outsem, rootsem, matsem,
):
    slabs = lax.axis_size("slab")
    chunks = X.shape[0]
    slab = lax.axis_index("slab")
    front = lax.axis_index("front")
    core = front % 2
    chip = front // 2
    cx = chip % RING
    cy = chip // RING

    def at(x, y, c):
        return (slab, (y * RING + x) * 2 + c)

    partner = at(cx, cy, 1 - core)
    x_next = at((cx + 1) % RING, cy, core)
    x_prev = at((cx + RING - 1) % RING, cy, core)
    y_next = at(cx, (cy + 1) % RING, core)
    y_prev = at(cx, (cy + RING - 1) % RING, core)
    z_next = ((slab + 1) % slabs, front)
    z_prev = ((slab + slabs - 1) % slabs, front)
    ways = ((x_next, x_prev), (y_next, y_prev))

    barrier = pltpu.get_barrier_semaphore()
    for device in (partner, x_next, x_prev, y_next, y_prev, z_next, z_prev):
        pl.semaphore_signal(barrier, inc=1, device_id=device, device_id_type=pl.DeviceIdType.MESH)

    def cols(k):
        return pl.ds(pl.multiple_of(k * C, C), C)

    def rhs_in(k):
        return pltpu.make_async_copy(rhs.at[0, :, :, :, cols(k)], X.at[k], insem.at[k])

    def root_rhs_in(k):
        return pltpu.make_async_copy(root_rhs.at[0, :, :, cols(k)], RR.at[k], rrsem.at[k])

    def sol_back(k):
        return pltpu.make_async_copy(X.at[k], sol_out.at[0, :, :, :, cols(k)], outsem.at[k])

    def root_back(k):
        return pltpu.make_async_copy(Y.at[k], root_out.at[0, :, :, cols(k)], rootsem.at[k])

    def matrices_in():
        return (
            pltpu.make_async_copy(inv_in, inv, matsem.at[0]),
            pltpu.make_async_copy(off_in, off, matsem.at[1]),
        )

    for k in range(chunks):
        rhs_in(k).start()
        if k == 0:
            for copy in matrices_in():
                copy.start()
    for k in range(chunks):
        root_rhs_in(k).start()

    def find(l, carry):
        f = owners[l]
        rx = (((f >> 1) & 3) - cx) & 3
        ry = ((f >> 3) - cy) & 3
        leaf_slot[l] = (((f & 1) + core) & 1) * SLOTS + rx * RING + ry
        return carry

    lax.fori_loop(0, LEAF, find, 0)

    def invert(q, carry):
        for cls in range(2):
            found = jnp.int32(0)
            for l in range(LEAF):
                found = jnp.where(leaf_slot[l] == cls * SLOTS + q, l + 1, found)
            present = jnp.minimum(found, 1)
            leaf = jnp.maximum(found - 1, 0)
            slot_leaf[cls * SLOTS + q] = leaf
            ids[cls, pl.ds(q, 1), :] = anc[0, pl.ds(leaf, 1), :] * present + (present - 1)
        return carry

    lax.fori_loop(0, SLOTS, invert, 0)
    for b in range(2):
        row = jnp.broadcast_to(coupling[:, b * B:(b + 1) * B], (B, B))
        cpl[pl.ds(b * B, B), :] = row.T

    def send(src, dst, k, m, device):
        return pltpu.make_async_remote_copy(
            src_ref=src, dst_ref=dst, send_sem=ssem.at[k, m], recv_sem=rsem.at[k, m],
            device_id=device, device_id_type=pl.DeviceIdType.MESH,
        )

    def ids_copy():
        return pltpu.make_async_remote_copy(
            src_ref=ids.at[1], dst_ref=IDR, send_sem=idsem.at[0], recv_sem=idsem.at[1],
            device_id=partner, device_id_type=pl.DeviceIdType.MESH,
        )

    def part_copy(k):
        return send(SND.at[k], RCV.at[k], k, 0, partner)

    def rs_copy(k, p, phase, m):
        nxt, prv = ways[p if phase == 0 else 1 - p]
        if phase == 0:
            src, mid, fin = E, A1, F1
        else:
            src, mid, fin = R1, A2, F2
        s, d, device = (
            (src.at[k, p, 2, 0], mid.at[k, p, 0], nxt),
            (src.at[k, p, 1, 1], fin.at[k, p, 0, 1], nxt),
            (src.at[k, p, 1, 0], fin.at[k, p, 0, 0], nxt),
            (src.at[k, p, 2, 1], mid.at[k, p, 1], prv),
            (src.at[k, p, 3, 0], fin.at[k, p, 1, 0], prv),
            (src.at[k, p, 3, 1], fin.at[k, p, 1, 1], prv),
        )[m]
        return send(s, d, k, 1 + phase * 12 + p * 6 + m, device)

    def sweep_copy(k, b):
        return send(G.at[k, :, 0, b, 0], Z.at[k, b], k, 25 + b, z_next)

    def ag_copy(k, p, phase, m):
        nxt, prv = ways[1 - p if phase == 0 else p]
        if phase == 0:
            def g(r, h):
                return G.at[k, p, 0, h, r]
        else:
            def g(r, h):
                return G.at[k, p, r, h]
        s, d, device = (
            (g(0, 0), g(3, 0), nxt),
            (g(0, 1), g(3, 1), nxt),
            (g(3, 0), g(2, 0), nxt),
            (g(0, 1), g(1, 1), prv),
            (g(0, 0), g(1, 0), prv),
            (g(1, 1), g(2, 1), prv),
        )[m]
        return send(s, d, k, 27 + phase * 12 + p * 6 + m, device)

    def pick_copy(k):
        return send(SND.at[k], RCB.at[k], k, 51, partner)

    @pl.when(slab == 0)
    def _():
        Z[...] = jnp.zeros_like(Z)

    pl.semaphore_wait(barrier, 7)
    ids_copy().start()

    for b in range(2):
        full = widened(root_inv[0, b, 0], root_inv[0, b, 1])
        high = full.astype(BF)
        AH[b] = high
        AL[b] = (full - high.astype(F32)).astype(BF)

    def fwd(k):
        @pl.when(k == 0)
        def _():
            for copy in matrices_in():
                copy.wait()

        rhs_in(k).wait()
        par = k % 2

        def leaves(g, carry):
            ls = [g * WIDE + i for i in range(WIDE)]
            v = [jnp.concatenate([X[k, 0, l], X[k, 1, l]], axis=0) for l in ls]
            f = [dot(widened(inv[0, l, 0], inv[0, l, 1]), a).astype(BF) for l, a in zip(ls, v)]
            w = [dot(widened(off[0, l, 0], off[0, l, 1]), a).astype(BF) for l, a in zip(ls, f)]
            for l, a, b in zip(ls, f, w):
                X[k, 0, l] = a[:B]
                X[k, 1, l] = a[B:]
                PART[par, l, 0] = b[:B]
                PART[par, l, 1] = b[B:]
            return carry

        lax.fori_loop(0, LEAF // WIDE, leaves, 0)

        def put(q, carry):
            SND[k, q] = PART[par, slot_leaf[SLOTS + q]]
            return carry

        lax.fori_loop(0, SLOTS, put, 0, unroll=2)
        part_copy(k).start()

    def setup_tables():
        ids_copy().wait_recv()

        def table(q, carry):
            both = jnp.concatenate([ids[0, pl.ds(q, 1), :], IDR[pl.ds(q, 1), :]], axis=1)
            rows = lax.broadcasted_iota(jnp.int32, (2 * B, 2 * B), 0)
            T[q] = jnp.where(rows == jnp.broadcast_to(both, (2 * B, 2 * B)), 1.0, 0.0).astype(BF)
            return carry

        lax.fori_loop(0, SLOTS, table, 0)

    def setup_transposed():
        def table(q, carry):
            TT[q] = T[q].astype(F32).T.astype(BF)
            OFFT[q] = widened(off[0, q, 0].astype(F32).T, off[0, q, 1].astype(F32).T).astype(BF)
            return carry

        lax.fori_loop(0, SLOTS, table, 0)

    def expand(k):
        part_copy(k).wait_recv()
        par = k % 2

        def slots(rx, carry):
            v = []
            for ry in range(RING):
                q = rx * RING + ry
                leaf = slot_leaf[q]
                mine = jnp.concatenate([PART[par, leaf, 0], PART[par, leaf, 1]], axis=1)
                other = jnp.concatenate([RCV[k, q, 0], RCV[k, q, 1]], axis=1)
                v.append(jnp.concatenate([mine, other], axis=0))
            e = [dot(T[rx * RING + ry], a).astype(BF) for ry, a in enumerate(v)]
            for ry, a in enumerate(e):
                E[k, 0, rx, 0, ry] = a[:B, :C]
                E[k, 0, rx, 1, ry] = a[B:, :C]
                E[k, 1, ry, 0, rx] = a[:B, C:]
                E[k, 1, ry, 1, rx] = a[B:, C:]
            return carry

        lax.fori_loop(0, RING, slots, 0)
        for m in (0, 3, 1, 4):
            for p in range(2):
                rs_copy(k, p, 0, m).start()

    def rs_relay_first(k):
        for m, r, h, d in ((0, 1, 0, 0), (3, 3, 1, 1)):
            for p in range(2):
                rs_copy(k, p, 0, m).wait_recv()
                for i in range(RING):
                    E[k, p, r, h, i] = (
                        E[k, p, r, h, i].astype(F32) + A1[k, p, d, i].astype(F32)
                    ).astype(BF)
                rs_copy(k, p, 0, 2 if d == 0 else 5).start()

    def rs_turn(k):
        for p in range(2):
            for m in (1, 4, 2, 5):
                rs_copy(k, p, 0, m).wait_recv()
            for r in (2, 1, 3, 0):
                for h in range(2):
                    R1[k, p, r, h] = (
                        E[k, p, 0, h, r].astype(F32)
                        + F1[k, p, 0, h, r].astype(F32)
                        + F1[k, p, 1, h, r].astype(F32)
                    ).astype(BF)
            for m in (0, 3, 1, 4):
                rs_copy(k, p, 1, m).start()

    def rs_relay_second(k):
        for m, r, h, d in ((0, 1, 0, 0), (3, 3, 1, 1)):
            for p in range(2):
                rs_copy(k, p, 1, m).wait_recv()
                R1[k, p, r, h] = (
                    R1[k, p, r, h].astype(F32) + A2[k, p, d].astype(F32)
                ).astype(BF)
                rs_copy(k, p, 1, 2 if d == 0 else 5).start()

    def sweep(k):
        root_rhs_in(k).wait()
        for p in range(2):
            for m in (1, 4, 2, 5):
                rs_copy(k, p, 1, m).wait_recv()
        for b in range(2):
            right = []
            for p in range(2):
                total = (
                    R1[k, p, 0, b].astype(F32)
                    + F2[k, p, 0, b].astype(F32)
                    + F2[k, p, 1, b].astype(F32)
                )
                right.append(RR[k, p, pl.ds(b * B, B), :].astype(F32) - total)

            @pl.when(slab > 0)
            def _():
                sweep_copy(k, b).wait_recv()

            scale = cpl[pl.ds(b * B, B), :]
            field = jnp.concatenate(
                [right[p] - scale * Z[k, b, p].astype(F32) for p in range(2)], axis=0
            )
            high = field.astype(BF)
            low = (field - high.astype(F32)).astype(BF)
            state = dot(AH[b], low) + dot(AL[b], high) + dot(AH[b], high)
            for p in range(2):
                piece = state[p * B:(p + 1) * B]
                G[k, p, 0, b, 0] = piece.astype(BF)
                Y[k, p, pl.ds(b * B, B), :] = piece

            @pl.when(slab < slabs - 1)
            def _():
                sweep_copy(k, b).start()

        root_back(k).start()

    def ag_send(k):
        for m in (0, 3, 1, 4):
            for p in range(2):
                ag_copy(k, p, 0, m).start()

    def ag_forward(k, phase):
        for m in (0, 3):
            for p in range(2):
                ag_copy(k, p, phase, m).wait_recv()
                ag_copy(k, p, phase, m + 2).start()

    def ag_turn(k):
        for p in range(2):
            for m in (1, 4, 2, 5):
                ag_copy(k, p, 0, m).wait_recv()
        for m in (0, 3, 1, 4):
            for p in range(2):
                ag_copy(k, p, 1, m).start()

    def pick(k):
        for p in range(2):
            for m in (1, 4, 2, 5):
                ag_copy(k, p, 1, m).wait_recv()
        part_copy(k).wait_send()

        def slots(rx, carry):
            v = []
            for ry in range(RING):
                top = jnp.concatenate([G[k, 0, rx, 0, ry], G[k, 1, ry, 0, rx]], axis=1)
                low = jnp.concatenate([G[k, 0, rx, 1, ry], G[k, 1, ry, 1, rx]], axis=1)
                v.append(jnp.concatenate([top, low], axis=0))
            e = [dot(TT[rx * RING + ry], a).astype(BF) for ry, a in enumerate(v)]
            for ry, a in enumerate(e):
                q = rx * RING + ry
                STAGE[k % 2, q, 0] = a[:B, :C]
                STAGE[k % 2, q, 1] = a[:B, C:]
                SND[k, q, 0] = a[B:, :C]
                SND[k, q, 1] = a[B:, C:]
            return carry

        lax.fori_loop(0, RING, slots, 0)
        pick_copy(k).start()

    def back(k):
        pick_copy(k).wait_recv()

        def put(q, carry):
            STAGE[k % 2, SLOTS + q] = RCB[k, q]
            return carry

        lax.fori_loop(0, SLOTS, put, 0, unroll=2)

        def leaves(g, carry):
            ls = [g * WIDE + i for i in range(WIDE)]
            ss = [leaf_slot[l] for l in ls]
            v = [jnp.concatenate([STAGE[k % 2, n, 0], STAGE[k % 2, n, 1]], axis=0) for n in ss]
            f = [jnp.concatenate([X[k, 0, l], X[k, 1, l]], axis=0).astype(F32) for l in ls]
            w = [dot(OFFT[l], a).astype(BF) for l, a in zip(ls, v)]
            u = [dot(widened(inv[0, l, 0], inv[0, l, 1]), a) for l, a in zip(ls, w)]
            for l, a, b in zip(ls, f, u):
                r = (a - b).astype(BF)
                X[k, 0, l] = r[:B]
                X[k, 1, l] = r[B:]
            return carry

        lax.fori_loop(0, LEAF // WIDE, leaves, 0)
        sol_back(k).start()

    lag = (slab * LAG_NUM + LAG_ADD) // LAG_DEN
    sw = 5 + lag
    g1 = jnp.maximum(GATHER[0], sw)
    g2 = jnp.maximum(GATHER[1], sw)
    g3 = jnp.maximum(GATHER[2], sw + 1)
    last = max(GATHER[2], 6 + ((slabs - 1) * LAG_NUM + LAG_ADD) // LAG_DEN)

    def step(j, carry):
        def run(op, shift, *rest):
            k = j - shift

            @pl.when((k >= 0) & (k < chunks))
            def _():
                op(k, *rest)

        run(fwd, 0)

        @pl.when(j == 1)
        def _():
            setup_tables()

        run(expand, 1)
        run(rs_relay_first, 2)

        @pl.when(j == 4)
        def _():
            setup_transposed()

        run(rs_turn, 3)
        run(rs_relay_second, 4)
        run(sweep, sw)
        run(ag_send, g1)
        run(ag_turn, g3)
        run(ag_forward, g2, 0)
        run(ag_forward, g3, 1)
        run(pick, g3 + 1)
        run(back, g3 + 2)
        return carry

    lax.fori_loop(0, chunks + last + 2, step, 0)

    ids_copy().wait_send()

    def drain(k, carry):
        sol_back(k).wait()
        root_back(k).wait()
        for phase in range(2):
            for p in range(2):
                for m in range(6):
                    rs_copy(k, p, phase, m).wait_send()
                    ag_copy(k, p, phase, m).wait_send()
        for b in range(2):
            @pl.when(slab < slabs - 1)
            def _():
                sweep_copy(k, b).wait_send()
        pick_copy(k).wait_send()
        return carry

    lax.fori_loop(0, chunks, drain, 0)


def body(leaf_rhs, leaf_inv, leaf_off, parent, ancestors, root_rhs, root_inv, coupling):
    owners = parent.reshape(LEAF)
    width = leaf_rhs.shape[-1]
    chunks = width // C
    vmem = pl.BlockSpec(memory_space=pltpu.VMEM)
    smem = pl.BlockSpec(memory_space=pltpu.SMEM)
    hbm = pl.BlockSpec(memory_space=pl.ANY)
    scratch = [
        pltpu.SMEM((2 * SLOTS,), jnp.int32),
        pltpu.SMEM((LEAF,), jnp.int32),
        pltpu.VMEM((2, SLOTS, B), jnp.int32),
        pltpu.VMEM((1, LEAF, 2, B, B), BF),
        pltpu.VMEM((1, LEAF, 2, B, B), BF),
        pltpu.VMEM((2 * B, C), F32),
        pltpu.VMEM((chunks, 2, LEAF, B, C), BF),
        pltpu.VMEM((2, LEAF, 2, B, C), BF),
        pltpu.VMEM((chunks, SLOTS, 2, B, C), BF),
        pltpu.VMEM((chunks, SLOTS, 2, B, C), BF),
        pltpu.VMEM((SLOTS, B), jnp.int32),
        pltpu.VMEM((SLOTS, 2 * B, 2 * B), BF),
        pltpu.VMEM((SLOTS, 2 * B, 2 * B), BF),
        pltpu.VMEM((LEAF, 2 * B, 2 * B), BF),
        pltpu.VMEM((chunks, 2, RING, 2, RING, B, C), BF),
        pltpu.VMEM((chunks, 2, 2, RING, B, C), BF),
        pltpu.VMEM((chunks, 2, 2, 2, RING, B, C), BF),
        pltpu.VMEM((chunks, 2, RING, 2, B, C), BF),
        pltpu.VMEM((chunks, 2, 2, B, C), BF),
        pltpu.VMEM((chunks, 2, 2, 2, B, C), BF),
        pltpu.VMEM((chunks, 2, 2 * B, C), BF),
        pltpu.VMEM((2, 2 * B, 2 * B), BF),
        pltpu.VMEM((2, 2 * B, 2 * B), BF),
        pltpu.VMEM((chunks, 2, 2, B, C), BF),
        pltpu.VMEM((chunks, 2, 2 * B, C), F32),
        pltpu.VMEM((chunks, 2, RING, 2, RING, B, C), BF),
        pltpu.VMEM((chunks, SLOTS, 2, B, C), BF),
        pltpu.VMEM((2, 2 * SLOTS, 2, B, C), BF),
        pltpu.SemaphoreType.DMA((chunks, MESSAGES)),
        pltpu.SemaphoreType.DMA((chunks, MESSAGES)),
        pltpu.SemaphoreType.DMA((2,)),
        pltpu.SemaphoreType.DMA((chunks,)),
        pltpu.SemaphoreType.DMA((chunks,)),
        pltpu.SemaphoreType.DMA((chunks,)),
        pltpu.SemaphoreType.DMA((chunks,)),
        pltpu.SemaphoreType.DMA((2,)),
    ]
    return pl.pallas_call(
        kernel,
        out_shape=(
            jax.ShapeDtypeStruct(leaf_rhs.shape, BF),
            jax.ShapeDtypeStruct(root_rhs.shape, F32),
        ),
        in_specs=[smem, hbm, hbm, hbm, vmem, hbm, vmem, vmem],
        out_specs=(hbm, hbm),
        scratch_shapes=scratch,
        compiler_params=pltpu.CompilerParams(
            collective_id=0, has_side_effects=True, vmem_limit_bytes=67043328
        ),
        name="sweep_all",
    )(owners, leaf_rhs, leaf_inv, leaf_off, ancestors, root_rhs, root_inv, coupling)


def solution(mesh):
    in_specs = (
        P("slab", None, "front", None, None),
        P("slab", "front", None, None, None),
        P("slab", "front", None, None, None),
        P("slab", "front", None),
        P("slab", "front", None),
        P("slab", None, "front", None),
        P("slab", "front", None, None, None),
        P("slab", "front"),
    )
    out_specs = (P("slab", None, "front", None, None), P("slab", None, "front", None))
    return jax.shard_map(body, mesh=mesh, in_specs=in_specs, out_specs=out_specs, check_vma=False)
```

```python
import jax
import jax.numpy as jnp
from jax import lax
from jax.experimental import pallas as pl
from jax.experimental.pallas import tpu as pltpu
from jax.sharding import PartitionSpec as P

BF = jnp.bfloat16
F32 = jnp.float32
B = 128
C = 128
LEAF = 16
RING = 4
SLOTS = RING * RING
MESSAGES = 54
HALF = SLOTS // 2
LAG_NUM, LAG_ADD, LAG_DEN = 2, 5, 7
GATHER = (5, 6, 8)
WIDE = 8


def dot(a, b):
    return jnp.dot(a, b, preferred_element_type=F32)


def widened(real, imag):
    top = jnp.concatenate([real, -imag], axis=1)
    low = jnp.concatenate([imag, real], axis=1)
    return jnp.concatenate([top, low], axis=0)


def kernel(
    owners, rhs, inv_in, off_in, anc, root_rhs, root_inv, coupling,
    sol_out, root_out,
    slot_leaf, leaf_slot, ids, inv, off, cpl,
    X, PART, SND, RCV, IDR, T, TT, OFFT, E, A1, F1, R1, A2, F2, RR, AH, AL, Z, Y, G, RCB, STAGE,
    ssem, rsem, idsem, insem, rrsem, outsem, rootsem, matsem,
):
    slabs = lax.axis_size("slab")
    chunks = X.shape[0]
    slab = lax.axis_index("slab")
    front = lax.axis_index("front")
    core = front % 2
    chip = front // 2
    cx = chip % RING
    cy = chip // RING

    def at(x, y, c):
        return (slab, (y * RING + x) * 2 + c)

    partner = at(cx, cy, 1 - core)
    x_next = at((cx + 1) % RING, cy, core)
    x_prev = at((cx + RING - 1) % RING, cy, core)
    y_next = at(cx, (cy + 1) % RING, core)
    y_prev = at(cx, (cy + RING - 1) % RING, core)
    z_next = ((slab + 1) % slabs, front)
    z_prev = ((slab + slabs - 1) % slabs, front)
    ways = ((x_next, x_prev), (y_next, y_prev))

    barrier = pltpu.get_barrier_semaphore()
    for device in (partner, x_next, x_prev, y_next, y_prev, z_next, z_prev):
        pl.semaphore_signal(barrier, inc=1, device_id=device, device_id_type=pl.DeviceIdType.MESH)

    def cols(k):
        return pl.ds(pl.multiple_of(k * C, C), C)

    def rhs_in(k):
        return pltpu.make_async_copy(rhs.at[0, :, :, :, cols(k)], X.at[k], insem.at[k])

    def root_rhs_in(k):
        return pltpu.make_async_copy(root_rhs.at[0, :, :, cols(k)], RR.at[k], rrsem.at[k])

    def sol_back(k):
        return pltpu.make_async_copy(X.at[k], sol_out.at[0, :, :, :, cols(k)], outsem.at[k])

    def root_back(k):
        return pltpu.make_async_copy(Y.at[k], root_out.at[0, :, :, cols(k)], rootsem.at[k])

    def matrices_in():
        return (
            pltpu.make_async_copy(inv_in, inv, matsem.at[0]),
            pltpu.make_async_copy(off_in, off, matsem.at[1]),
        )

    for k in range(chunks):
        rhs_in(k).start()
        if k == 0:
            for copy in matrices_in():
                copy.start()
    for k in range(chunks):
        root_rhs_in(k).start()

    def find(l, carry):
        f = owners[l]
        rx = (((f >> 1) & 3) - cx) & 3
        ry = ((f >> 3) - cy) & 3
        leaf_slot[l] = (((f & 1) + core) & 1) * SLOTS + rx * RING + ry
        return carry

    lax.fori_loop(0, LEAF, find, 0)

    def invert(q, carry):
        for cls in range(2):
            found = jnp.int32(0)
            for l in range(LEAF):
                found = jnp.where(leaf_slot[l] == cls * SLOTS + q, l + 1, found)
            present = jnp.minimum(found, 1)
            leaf = jnp.maximum(found - 1, 0)
            slot_leaf[cls * SLOTS + q] = leaf
            ids[cls, pl.ds(q, 1), :] = anc[0, pl.ds(leaf, 1), :] * present + (present - 1)
        return carry

    lax.fori_loop(0, SLOTS, invert, 0)
    for b in range(2):
        row = jnp.broadcast_to(coupling[:, b * B:(b + 1) * B], (B, B))
        cpl[pl.ds(b * B, B), :] = row.T

    def send(src, dst, k, m, device):
        return pltpu.make_async_remote_copy(
            src_ref=src, dst_ref=dst, send_sem=ssem.at[k, m], recv_sem=rsem.at[k, m],
            device_id=device, device_id_type=pl.DeviceIdType.MESH,
        )

    def ids_copy():
        return pltpu.make_async_remote_copy(
            src_ref=ids.at[1], dst_ref=IDR, send_sem=idsem.at[0], recv_sem=idsem.at[1],
            device_id=partner, device_id_type=pl.DeviceIdType.MESH,
        )

    def part_copy(k, h):
        some = pl.ds(h * HALF, HALF)
        return send(SND.at[k, some], RCV.at[k, some], k, (0, 52)[h], partner)

    def rs_copy(k, p, phase, m):
        nxt, prv = ways[p if phase == 0 else 1 - p]
        if phase == 0:
            src, mid, fin = E, A1, F1
        else:
            src, mid, fin = R1, A2, F2
        s, d, device = (
            (src.at[k, p, 2, 0], mid.at[k, p, 0], nxt),
            (src.at[k, p, 1, 1], fin.at[k, p, 0, 1], nxt),
            (src.at[k, p, 1, 0], fin.at[k, p, 0, 0], nxt),
            (src.at[k, p, 2, 1], mid.at[k, p, 1], prv),
            (src.at[k, p, 3, 0], fin.at[k, p, 1, 0], prv),
            (src.at[k, p, 3, 1], fin.at[k, p, 1, 1], prv),
        )[m]
        return send(s, d, k, 1 + phase * 12 + p * 6 + m, device)

    def sweep_copy(k, b):
        return send(G.at[k, :, 0, b, 0], Z.at[k, b], k, 25 + b, z_next)

    def ag_copy(k, p, phase, m):
        nxt, prv = ways[1 - p if phase == 0 else p]
        if phase == 0:
            def g(r, h):
                return G.at[k, p, 0, h, r]
        else:
            def g(r, h):
                return G.at[k, p, r, h]
        s, d, device = (
            (g(0, 0), g(3, 0), nxt),
            (g(0, 1), g(3, 1), nxt),
            (g(3, 0), g(2, 0), nxt),
            (g(0, 1), g(1, 1), prv),
            (g(0, 0), g(1, 0), prv),
            (g(1, 1), g(2, 1), prv),
        )[m]
        return send(s, d, k, 27 + phase * 12 + p * 6 + m, device)

    def pick_copy(k, h):
        some = pl.ds(h * HALF, HALF)
        return send(SND.at[k, some], RCB.at[k, some], k, (51, 53)[h], partner)

    @pl.when(slab == 0)
    def _():
        Z[...] = jnp.zeros_like(Z)

    pl.semaphore_wait(barrier, 7)
    ids_copy().start()

    for b in range(2):
        full = widened(root_inv[0, b, 0], root_inv[0, b, 1])
        high = full.astype(BF)
        AH[b] = high
        AL[b] = (full - high.astype(F32)).astype(BF)

    def fwd(k):
        @pl.when(k == 0)
        def _():
            for copy in matrices_in():
                copy.wait()

        rhs_in(k).wait()
        par = k % 2

        def leaves(g, carry):
            ls = [g * WIDE + i for i in range(WIDE)]
            v = [jnp.concatenate([X[k, 0, l], X[k, 1, l]], axis=0) for l in ls]
            f = [dot(widened(inv[0, l, 0], inv[0, l, 1]), a).astype(BF) for l, a in zip(ls, v)]
            w = [dot(widened(off[0, l, 0], off[0, l, 1]), a).astype(BF) for l, a in zip(ls, f)]
            for l, a, b in zip(ls, f, w):
                X[k, 0, l] = a[:B]
                X[k, 1, l] = a[B:]
                PART[par, l, 0] = b[:B]
                PART[par, l, 1] = b[B:]
            return carry

        lax.fori_loop(0, LEAF // WIDE, leaves, 0)

        def put(q, carry):
            SND[k, q] = PART[par, slot_leaf[SLOTS + q]]
            return carry

        for h in range(2):
            lax.fori_loop(h * HALF, (h + 1) * HALF, put, 0, unroll=2)
            part_copy(k, h).start()

    def setup_tables():
        ids_copy().wait_recv()

        def table(q, carry):
            both = jnp.concatenate([ids[0, pl.ds(q, 1), :], IDR[pl.ds(q, 1), :]], axis=1)
            rows = lax.broadcasted_iota(jnp.int32, (2 * B, 2 * B), 0)
            T[q] = jnp.where(rows == jnp.broadcast_to(both, (2 * B, 2 * B)), 1.0, 0.0).astype(BF)
            return carry

        lax.fori_loop(0, SLOTS, table, 0)

    def setup_transposed():
        def table(q, carry):
            TT[q] = T[q].astype(F32).T.astype(BF)
            OFFT[q] = widened(off[0, q, 0].astype(F32).T, off[0, q, 1].astype(F32).T).astype(BF)
            return carry

        lax.fori_loop(0, SLOTS, table, 0)

    def expand(k):
        par = k % 2

        def slots(rx, carry):
            v = []
            for ry in range(RING):
                q = rx * RING + ry
                leaf = slot_leaf[q]
                mine = jnp.concatenate([PART[par, leaf, 0], PART[par, leaf, 1]], axis=1)
                other = jnp.concatenate([RCV[k, q, 0], RCV[k, q, 1]], axis=1)
                v.append(jnp.concatenate([mine, other], axis=0))
            e = [dot(T[rx * RING + ry], a).astype(BF) for ry, a in enumerate(v)]
            for ry, a in enumerate(e):
                E[k, 0, rx, 0, ry] = a[:B, :C]
                E[k, 0, rx, 1, ry] = a[B:, :C]
                E[k, 1, ry, 0, rx] = a[:B, C:]
                E[k, 1, ry, 1, rx] = a[B:, C:]
            return carry

        for h in range(2):
            part_copy(k, h).wait_recv()
            lax.fori_loop(h * 2, h * 2 + 2, slots, 0)
        for m in (0, 3, 1, 4):
            for p in range(2):
                rs_copy(k, p, 0, m).start()

    def rs_relay_first(k):
        for m, r, h, d in ((0, 1, 0, 0), (3, 3, 1, 1)):
            for p in range(2):
                rs_copy(k, p, 0, m).wait_recv()
                for i in range(RING):
                    E[k, p, r, h, i] = (
                        E[k, p, r, h, i].astype(F32) + A1[k, p, d, i].astype(F32)
                    ).astype(BF)
                rs_copy(k, p, 0, 2 if d == 0 else 5).start()

    def rs_turn(k):
        for p in range(2):
            for m in (1, 4, 2, 5):
                rs_copy(k, p, 0, m).wait_recv()
            for r in (2, 1, 3, 0):
                for h in range(2):
                    R1[k, p, r, h] = (
                        E[k, p, 0, h, r].astype(F32)
                        + F1[k, p, 0, h, r].astype(F32)
                        + F1[k, p, 1, h, r].astype(F32)
                    ).astype(BF)
            for m in (0, 3, 1, 4):
                rs_copy(k, p, 1, m).start()

    def rs_relay_second(k):
        for m, r, h, d in ((0, 1, 0, 0), (3, 3, 1, 1)):
            for p in range(2):
                rs_copy(k, p, 1, m).wait_recv()
                R1[k, p, r, h] = (
                    R1[k, p, r, h].astype(F32) + A2[k, p, d].astype(F32)
                ).astype(BF)
                rs_copy(k, p, 1, 2 if d == 0 else 5).start()

    def sweep(k):
        root_rhs_in(k).wait()
        for p in range(2):
            for m in (1, 4, 2, 5):
                rs_copy(k, p, 1, m).wait_recv()
        right = [
            RR[k, p, pl.ds(b * B, B), :].astype(F32)
            - (
                R1[k, p, 0, b].astype(F32)
                + F2[k, p, 0, b].astype(F32)
                + F2[k, p, 1, b].astype(F32)
            )
            for b in range(2)
            for p in range(2)
        ]
        states = []
        for b in range(2):
            scale = cpl[pl.ds(b * B, B), :]

            @pl.when(slab > 0)
            def _():
                sweep_copy(k, b).wait_recv()

            field = jnp.concatenate(
                [right[2 * b + p] - scale * Z[k, b, p].astype(F32) for p in range(2)], axis=0
            )
            high = field.astype(BF)
            low = (field - high.astype(F32)).astype(BF)
            state = dot(AH[b], low) + dot(AL[b], high) + dot(AH[b], high)
            states.append(state)
            for p in range(2):
                G[k, p, 0, b, 0] = state[p * B:(p + 1) * B].astype(BF)

            @pl.when(slab < slabs - 1)
            def _():
                sweep_copy(k, b).start()

        for b in range(2):
            for p in range(2):
                Y[k, p, pl.ds(b * B, B), :] = states[b][p * B:(p + 1) * B]
        root_back(k).start()

    def ag_send(k):
        for m in (0, 3, 1, 4):
            for p in range(2):
                ag_copy(k, p, 0, m).start()

    def ag_forward(k, phase):
        for m in (0, 3):
            for p in range(2):
                ag_copy(k, p, phase, m).wait_recv()
                ag_copy(k, p, phase, m + 2).start()

    def ag_turn(k):
        for p in range(2):
            for m in (1, 4, 2, 5):
                ag_copy(k, p, 0, m).wait_recv()
        for m in (0, 3, 1, 4):
            for p in range(2):
                ag_copy(k, p, 1, m).start()

    def pick(k):
        for p in range(2):
            for m in (1, 4, 2, 5):
                ag_copy(k, p, 1, m).wait_recv()
        for h in range(2):
            part_copy(k, h).wait_send()

        def slots(rx, carry):
            v = []
            for ry in range(RING):
                top = jnp.concatenate([G[k, 0, rx, 0, ry], G[k, 1, ry, 0, rx]], axis=1)
                low = jnp.concatenate([G[k, 0, rx, 1, ry], G[k, 1, ry, 1, rx]], axis=1)
                v.append(jnp.concatenate([top, low], axis=0))
            e = [dot(TT[rx * RING + ry], a).astype(BF) for ry, a in enumerate(v)]
            for ry, a in enumerate(e):
                q = rx * RING + ry
                STAGE[k % 2, q, 0] = a[:B, :C]
                STAGE[k % 2, q, 1] = a[:B, C:]
                SND[k, q, 0] = a[B:, :C]
                SND[k, q, 1] = a[B:, C:]
            return carry

        for h in range(2):
            lax.fori_loop(h * 2, h * 2 + 2, slots, 0)
            pick_copy(k, h).start()

    def back(k):
        def put(q, carry):
            STAGE[k % 2, SLOTS + q] = RCB[k, q]
            return carry

        for h in range(2):
            pick_copy(k, h).wait_recv()
            lax.fori_loop(h * HALF, (h + 1) * HALF, put, 0, unroll=2)

        def leaves(g, carry):
            ls = [g * WIDE + i for i in range(WIDE)]
            ss = [leaf_slot[l] for l in ls]
            v = [jnp.concatenate([STAGE[k % 2, n, 0], STAGE[k % 2, n, 1]], axis=0) for n in ss]
            f = [jnp.concatenate([X[k, 0, l], X[k, 1, l]], axis=0).astype(F32) for l in ls]
            w = [dot(OFFT[l], a).astype(BF) for l, a in zip(ls, v)]
            u = [dot(widened(inv[0, l, 0], inv[0, l, 1]), a) for l, a in zip(ls, w)]
            for l, a, b in zip(ls, f, u):
                r = (a - b).astype(BF)
                X[k, 0, l] = r[:B]
                X[k, 1, l] = r[B:]
            return carry

        lax.fori_loop(0, LEAF // WIDE, leaves, 0)
        sol_back(k).start()

    lag = (slab * LAG_NUM + LAG_ADD) // LAG_DEN
    sw = 5 + lag
    g1 = jnp.maximum(GATHER[0], sw)
    g2 = jnp.maximum(GATHER[1], sw)
    g3 = jnp.maximum(GATHER[2], sw + 1)
    last = max(GATHER[2], 6 + ((slabs - 1) * LAG_NUM + LAG_ADD) // LAG_DEN)

    def step(j, carry):
        def run(op, shift, *rest):
            k = j - shift

            @pl.when((k >= 0) & (k < chunks))
            def _():
                op(k, *rest)

        run(fwd, 0)

        @pl.when(j == 1)
        def _():
            setup_tables()

        run(expand, 1)
        run(rs_relay_first, 2)

        @pl.when(j == 4)
        def _():
            setup_transposed()

        run(rs_turn, 3)
        run(rs_relay_second, 4)
        run(sweep, sw)
        run(ag_send, g1)
        run(ag_turn, g3)
        run(ag_forward, g2, 0)
        run(ag_forward, g3, 1)
        run(pick, g3 + 1)
        run(back, g3 + 2)
        return carry

    lax.fori_loop(0, chunks + last + 2, step, 0)

    ids_copy().wait_send()

    def drain(k, carry):
        sol_back(k).wait()
        root_back(k).wait()
        for phase in range(2):
            for p in range(2):
                for m in range(6):
                    rs_copy(k, p, phase, m).wait_send()
                    ag_copy(k, p, phase, m).wait_send()
        for b in range(2):
            @pl.when(slab < slabs - 1)
            def _():
                sweep_copy(k, b).wait_send()
        for h in range(2):
            pick_copy(k, h).wait_send()
        return carry

    lax.fori_loop(0, chunks, drain, 0)


def body(leaf_rhs, leaf_inv, leaf_off, parent, ancestors, root_rhs, root_inv, coupling):
    owners = parent.reshape(LEAF)
    width = leaf_rhs.shape[-1]
    chunks = width // C
    vmem = pl.BlockSpec(memory_space=pltpu.VMEM)
    smem = pl.BlockSpec(memory_space=pltpu.SMEM)
    hbm = pl.BlockSpec(memory_space=pl.ANY)
    scratch = [
        pltpu.SMEM((2 * SLOTS,), jnp.int32),
        pltpu.SMEM((LEAF,), jnp.int32),
        pltpu.VMEM((2, SLOTS, B), jnp.int32),
        pltpu.VMEM((1, LEAF, 2, B, B), BF),
        pltpu.VMEM((1, LEAF, 2, B, B), BF),
        pltpu.VMEM((2 * B, C), F32),
        pltpu.VMEM((chunks, 2, LEAF, B, C), BF),
        pltpu.VMEM((2, LEAF, 2, B, C), BF),
        pltpu.VMEM((chunks, SLOTS, 2, B, C), BF),
        pltpu.VMEM((chunks, SLOTS, 2, B, C), BF),
        pltpu.VMEM((SLOTS, B), jnp.int32),
        pltpu.VMEM((SLOTS, 2 * B, 2 * B), BF),
        pltpu.VMEM((SLOTS, 2 * B, 2 * B), BF),
        pltpu.VMEM((LEAF, 2 * B, 2 * B), BF),
        pltpu.VMEM((chunks, 2, RING, 2, RING, B, C), BF),
        pltpu.VMEM((chunks, 2, 2, RING, B, C), BF),
        pltpu.VMEM((chunks, 2, 2, 2, RING, B, C), BF),
        pltpu.VMEM((chunks, 2, RING, 2, B, C), BF),
        pltpu.VMEM((chunks, 2, 2, B, C), BF),
        pltpu.VMEM((chunks, 2, 2, 2, B, C), BF),
        pltpu.VMEM((chunks, 2, 2 * B, C), BF),
        pltpu.VMEM((2, 2 * B, 2 * B), BF),
        pltpu.VMEM((2, 2 * B, 2 * B), BF),
        pltpu.VMEM((chunks, 2, 2, B, C), BF),
        pltpu.VMEM((chunks, 2, 2 * B, C), F32),
        pltpu.VMEM((chunks, 2, RING, 2, RING, B, C), BF),
        pltpu.VMEM((chunks, SLOTS, 2, B, C), BF),
        pltpu.VMEM((2, 2 * SLOTS, 2, B, C), BF),
        pltpu.SemaphoreType.DMA((chunks, MESSAGES)),
        pltpu.SemaphoreType.DMA((chunks, MESSAGES)),
        pltpu.SemaphoreType.DMA((2,)),
        pltpu.SemaphoreType.DMA((chunks,)),
        pltpu.SemaphoreType.DMA((chunks,)),
        pltpu.SemaphoreType.DMA((chunks,)),
        pltpu.SemaphoreType.DMA((chunks,)),
        pltpu.SemaphoreType.DMA((2,)),
    ]
    return pl.pallas_call(
        kernel,
        out_shape=(
            jax.ShapeDtypeStruct(leaf_rhs.shape, BF),
            jax.ShapeDtypeStruct(root_rhs.shape, F32),
        ),
        in_specs=[smem, hbm, hbm, hbm, vmem, hbm, vmem, vmem],
        out_specs=(hbm, hbm),
        scratch_shapes=scratch,
        compiler_params=pltpu.CompilerParams(
            collective_id=0, has_side_effects=True, vmem_limit_bytes=67043328
        ),
        name="sweep_all",
    )(owners, leaf_rhs, leaf_inv, leaf_off, ancestors, root_rhs, root_inv, coupling)


def solution(mesh):
    in_specs = (
        P("slab", None, "front", None, None),
        P("slab", "front", None, None, None),
        P("slab", "front", None, None, None),
        P("slab", "front", None),
        P("slab", "front", None),
        P("slab", None, "front", None),
        P("slab", "front", None, None, None),
        P("slab", "front"),
    )
    out_specs = (P("slab", None, "front", None, None), P("slab", None, "front", None))
    return jax.shard_map(body, mesh=mesh, in_specs=in_specs, out_specs=out_specs, check_vma=False)
```
